512 devices in a mesh: lat: 8 (over z_lo), lon: 16 (over x, z_hi, core), mp: 4 (over y).
Axes of the slice: x: 4, y: 4, z: 16 (z_hi: 2, z_lo: 8; z = z_hi * 8 + z_lo), core: 2. Of those that a mesh axis runs over, the one named last changes fastest.
Arguments:
- sharp_resolution_vectors: bfloat16 [2, 128, 256, 512], P(None, 'lat', 'lon'), may hold values from -6 to 6
- queries_keys_weights: bfloat16 [512, 2, 512], P(None, None, 'mp'), may hold values from -0.03125 to 0.03125
- values_weights: bfloat16 [512, 512], P(None, 'mp'), may hold values from -0.25 to 0.25
- attn_result_weights: bfloat16 [512, 512], P('mp'), may hold values from -0.75 to 0.75
- score_factors_by_lane: float32 [8], replicated, may hold values from 1 to 8
- tile_merging_weights: bfloat16 [2048, 1024], P('lon', 'mp'), may hold values from -0.125 to 0.125
- shrunk_dense_first: bfloat16 [1024, 4096], P('lon', 'mp'), may hold values from -0.1875 to 0.1875
- shrunk_dense_second: bfloat16 [4096, 1024], P('mp', 'lon'), may hold values from -0.09375 to 0.09375
- tile_unfolding_weights: bfloat16 [1024, 2048], P('lon', 'mp'), may hold values from -0.1875 to 0.1875
- result_gradient: bfloat16 [2, 128, 256, 512], P(None, 'lat', ('lon', 'mp')), may hold values from -6 to 6
Outputs:
- output: bfloat16 [2, 128, 256, 512], P(None, 'lat', ('lon', 'mp'))
- fine_grad: bfloat16 [2, 128, 256, 512], P(None, 'lat', ('lon', 'mp'))
The draws below stay inside these ranges and needn't reach their ends.
All inputs are finite; a program needn't handle non-finite values.
Results may differ from the reference program's by a relative error of at most 0.02.
Values may be sent and summed in bfloat16 or wider, within the bound.
No kernel may reach another device: no remote copies, remote signals or barrier semaphores. Data moves between devices by JAX's collectives and lax.ppermute only.
A program may use at most 128 MiB of HBM per device.

```python
import math
import jax
import jax.numpy as jnp
from jax import lax

MODEL_BREADTH = 512
SHARP_ATTN_LANES = 8
HID = 4096
TILE_SIDE_CELLS = 8
LEVELS = 2
HEAD = 64
NLAT = 128
NLON = 256


def shard_levels(key, extent, shards, smallest, top_value):
    gain = 1.0
    for dim, blocks in shards:
        steps = jax.random.uniform(jax.random.fold_in(jax.random.fold_in(key, 6), dim), (blocks,), jnp.float32, smallest / len(shards), top_value / len(shards))
        gain = gain * jnp.repeat(jnp.exp(steps), extent[dim] // blocks).reshape((-1,) + (1,) * (len(extent) - 1 - dim))
    return gain


def bell_draw(stream_key, shape, deviation, limit, shards=(), held_as=jnp.bfloat16):
    result = jax.random.normal(stream_key, shape, jnp.float32) * deviation
    if len(shards) > 0:
        result = shard_levels(stream_key, shape, shards, -0.22, 0.18) * result
    return jnp.clip(result, min=-limit, max=limit).astype(held_as)


def setup_inputs(seed: int = 0) -> dict:
    key_of = jax.random.split(jax.random.key(seed), 11)
    return {
        "sharp_resolution_vectors": bell_draw(key_of[0], (LEVELS, NLAT, NLON, MODEL_BREADTH), 1.0, 6.0, ((1, 8), (2, 16))),
        "queries_keys_weights": bell_draw(key_of[1], (MODEL_BREADTH, 2, MODEL_BREADTH), (HEAD * MODEL_BREADTH) ** -0.5, 0.03125, ((2, 4),)),
        "values_weights": bell_draw(key_of[2], (MODEL_BREADTH, MODEL_BREADTH), MODEL_BREADTH ** -0.5, 0.25, ((1, 4),)),
        "attn_result_weights": bell_draw(key_of[3], (MODEL_BREADTH, MODEL_BREADTH), HEAD ** -0.5, 0.75, ((0, 4),)),
        "score_factors_by_lane": jnp.clip(jnp.exp(jax.random.uniform(key_of[4], (SHARP_ATTN_LANES,), jnp.float32, math.log(1.0), math.log(8.0))), 1.0, 8.0),
        "tile_merging_weights": bell_draw(key_of[5], (4 * MODEL_BREADTH, 2 * MODEL_BREADTH), (4 * MODEL_BREADTH) ** -0.5, 0.125, ((0, 16), (1, 4))),
        "shrunk_dense_first": bell_draw(key_of[6], (2 * MODEL_BREADTH, HID), (2 * MODEL_BREADTH) ** -0.5, 0.1875, ((0, 16), (1, 4))),
        "shrunk_dense_second": bell_draw(key_of[7], (HID, 2 * MODEL_BREADTH), HID ** -0.5, 0.09375, ((0, 4), (1, 16))),
        "tile_unfolding_weights": bell_draw(key_of[8], (2 * MODEL_BREADTH, 4 * MODEL_BREADTH), (2 * MODEL_BREADTH) ** -0.5, 0.1875, ((0, 16), (1, 4))),
        "result_gradient": bell_draw(key_of[9], (LEVELS, NLAT, NLON, MODEL_BREADTH), 1.0, 6.0, ((1, 8), (2, 64))),
    }


epsilon = 1e-05

def layer_norm(inputs):
    values = inputs.astype(jnp.float32)
    center = values - lax.optimization_barrier(jnp.mean(values, -1, keepdims=True))
    spread = lax.optimization_barrier(jnp.mean(center * center, -1, keepdims=True))
    return center * lax.rsqrt(spread + epsilon)

def norm_round(inputs):
    return layer_norm(inputs).astype(jnp.bfloat16)

def activate(inputs):
    return jax.nn.gelu(inputs.astype(jnp.float32)).astype(jnp.bfloat16)

def unit_rows(tensor):
    values = tensor.astype(jnp.float32)
    length = jnp.sqrt(lax.optimization_barrier(jnp.sum(values * values, -1, keepdims=True)))
    return (values / jnp.maximum(length, 1.0)).astype(jnp.bfloat16)

def window_attention(query_rows, key_rows, value_rows, scales, allowed):
    query_unit = lax.optimization_barrier(unit_rows(query_rows)).astype(jnp.float32)
    key_unit = lax.optimization_barrier(unit_rows(key_rows)).astype(jnp.float32)
    scores = scales[None, :, None, None] * jnp.einsum('bthe,bshe->bhts', query_unit, key_unit, precision=lax.Precision.HIGHEST)
    weights_raw = jnp.where(allowed[:, None], jnp.exp(scores), 0.0)
    weights = lax.optimization_barrier((weights_raw / lax.optimization_barrier(jnp.sum(weights_raw, -1, keepdims=True))).astype(jnp.bfloat16))
    weighted_sum_vectors = jnp.einsum('bhts,bshe->bthe', weights.astype(jnp.float32), value_rows.astype(jnp.float32), precision=lax.Precision.HIGHEST)
    return weighted_sum_vectors.astype(jnp.bfloat16)

def to_windows(tensor):
    levels, row_count, column_count, depth = tensor.shape
    tensor = tensor.reshape(levels, row_count // TILE_SIDE_CELLS, TILE_SIDE_CELLS, column_count // TILE_SIDE_CELLS, TILE_SIDE_CELLS, depth).transpose(1, 3, 0, 2, 4, 5)
    return tensor.reshape(row_count // TILE_SIDE_CELLS, column_count // TILE_SIDE_CELLS, levels * TILE_SIDE_CELLS * TILE_SIDE_CELLS, depth)

def from_windows(tensor, levels):
    row_blocks, column_blocks, window_size, depth = tensor.shape
    tensor = tensor.reshape(row_blocks, column_blocks, levels, TILE_SIDE_CELLS, TILE_SIDE_CELLS, depth).transpose(2, 0, 3, 1, 4, 5)
    return tensor.reshape(levels, row_blocks * TILE_SIDE_CELLS, column_blocks * TILE_SIDE_CELLS, depth)

def tile_normalized_averager(stacked, scales, shifted_zone_marks):
    levels = stacked.shape[0]
    heads = scales.shape[0]
    width = stacked.shape[3] // 3
    windows = to_windows(stacked)
    row_blocks, column_blocks, window_size = windows.shape[:3]
    window_count = row_blocks * column_blocks

    def select_part(part_index):
        return windows[..., part_index * width:(part_index + 1) * width].reshape(window_count, window_size, heads, width // heads)
    token_label = jnp.broadcast_to(shifted_zone_marks.reshape(row_blocks, 1, TILE_SIDE_CELLS, 1), (row_blocks, levels, TILE_SIDE_CELLS, TILE_SIDE_CELLS)).reshape(row_blocks, window_size)
    allowed = token_label[:, :, None] == token_label[:, None, :]
    allowed = jnp.broadcast_to(allowed[:, None], (row_blocks, column_blocks, window_size, window_size)).reshape(window_count, window_size, window_size)
    weighted_sum_vectors = window_attention(select_part(0), select_part(1), select_part(2), scales, allowed)
    return from_windows(weighted_sum_vectors.reshape(row_blocks, column_blocks, window_size, width), levels)

def combined_normalizer(latent_finer_state):
    levels, row_count, column_count, width = latent_finer_state.shape
    grouped = latent_finer_state.reshape(levels, row_count // 2, 2, column_count // 2, 2, width).transpose(0, 1, 3, 2, 4, 5)
    grouped = grouped.reshape(levels, row_count // 2, column_count // 2, 4 * width)
    return layer_norm(grouped).astype(jnp.bfloat16)

def hourglass_single_pass(sharp_resolution_vectors, queries_keys_weights, values_weights, attn_result_weights, score_factors_by_lane, tile_merging_weights, shrunk_dense_first, shrunk_dense_second, tile_unfolding_weights):
    half_win = TILE_SIDE_CELLS // 2
    joined = jnp.concatenate([queries_keys_weights.reshape(MODEL_BREADTH, 2 * MODEL_BREADTH), values_weights], 1)
    rolled = jnp.roll(sharp_resolution_vectors, (-half_win, -half_win), axis=(1, 2))
    stacked = jnp.dot(norm_round(rolled), joined, preferred_element_type=jnp.float32).astype(jnp.bfloat16)
    position = jnp.arange(NLAT, dtype=jnp.int32)
    shifted_zone_marks = (position >= NLAT - TILE_SIDE_CELLS).astype(jnp.int32) + (position >= NLAT - half_win).astype(jnp.int32)
    attentive_sequence_blocks = NLAT // TILE_SIDE_CELLS
    north_south_slices = stacked.reshape(LEVELS, attentive_sequence_blocks, TILE_SIDE_CELLS, NLON, 3 * MODEL_BREADTH).transpose(1, 0, 2, 3, 4)
    weighted_sum_vectors = lax.map(lambda learned_weights_set: tile_normalized_averager(learned_weights_set[0], score_factors_by_lane, learned_weights_set[1]), (north_south_slices, shifted_zone_marks.reshape(attentive_sequence_blocks, TILE_SIDE_CELLS)))
    weighted_sum_vectors = weighted_sum_vectors.transpose(1, 0, 2, 3, 4).reshape(LEVELS, NLAT, NLON, MODEL_BREADTH)
    mixed_back = jnp.roll(weighted_sum_vectors, (half_win, half_win), axis=(1, 2))
    latent_finer_state = (sharp_resolution_vectors.astype(jnp.float32) + jnp.dot(mixed_back, attn_result_weights, preferred_element_type=jnp.float32)).astype(jnp.bfloat16)
    reduced_level = jnp.dot(combined_normalizer(latent_finer_state), tile_merging_weights, preferred_element_type=jnp.float32).astype(jnp.bfloat16)
    inner = jnp.dot(norm_round(reduced_level), shrunk_dense_first, preferred_element_type=jnp.float32).astype(jnp.bfloat16)
    coarse_out = (reduced_level.astype(jnp.float32) + jnp.dot(activate(inner), shrunk_dense_second, preferred_element_type=jnp.float32)).astype(jnp.bfloat16)
    expanded = jnp.dot(coarse_out, tile_unfolding_weights, preferred_element_type=jnp.float32).astype(jnp.bfloat16)
    expanded = expanded.reshape(LEVELS, NLAT // 2, NLON // 2, 2, 2, MODEL_BREADTH).transpose(0, 1, 3, 2, 4, 5).reshape(LEVELS, NLAT, NLON, MODEL_BREADTH)
    return (latent_finer_state.astype(jnp.float32) + expanded.astype(jnp.float32)).astype(jnp.bfloat16)

def reference(sharp_resolution_vectors, queries_keys_weights, values_weights, attn_result_weights, score_factors_by_lane, tile_merging_weights, shrunk_dense_first, shrunk_dense_second, tile_unfolding_weights, result_gradient):

    def forward(received_vectors):
        return hourglass_single_pass(received_vectors, queries_keys_weights, values_weights, attn_result_weights, score_factors_by_lane, tile_merging_weights, shrunk_dense_first, shrunk_dense_second, tile_unfolding_weights)
    output, pull_back = jax.vjp(forward, sharp_resolution_vectors)
    fine_grad = pull_back(result_gradient)[0]
    return (output, fine_grad)
```

```python
import jax
import jax.numpy as jnp
import numpy as np
from jax import lax
from jax.experimental import pallas as pl
from jax.experimental.pallas import tpu as pltpu
from jax.sharding import Mesh, PartitionSpec as P

BF, F32 = jnp.bfloat16, jnp.float32
EPS = 1e-05
LON = ("x", "zh", "core")
LONMP = LON + ("mp",)
ALL = ("lat",) + LONMP


def dot(a, b, ca=1, cb=0):
    return lax.dot_general(a, b, (((ca,), (cb,)), ((), ())), preferred_element_type=F32)


def to_all(value, axis):
    n = lax.axis_size(axis)
    return lax.all_to_all(
        jnp.broadcast_to(value[None], (n, *value.shape)), axis, 0, 0, tiled=True
    )


def swap(value, axis):
    return lax.all_to_all(value, axis, 0, 0, tiled=True)


def call(body, outs, scratch=(), n_scalar=0, n_in=0):
    specs = [pl.BlockSpec(memory_space=pltpu.SMEM)] * n_scalar + [
        pl.BlockSpec(memory_space=pltpu.VMEM)
    ] * n_in
    many = isinstance(outs, (list, tuple))
    ospecs = [pl.BlockSpec(memory_space=pltpu.VMEM)] * (len(outs) if many else 1)
    return pl.pallas_call(
        body,
        out_shape=outs,
        in_specs=specs,
        out_specs=ospecs if many else ospecs[0],
        scratch_shapes=list(scratch),
        compiler_params=pltpu.CompilerParams(vmem_limit_bytes=48 << 20),
    )


def arr(*shape, dtype=BF):
    return jax.ShapeDtypeStruct(shape, dtype)


def norm_parts(values, width):
    total = sum(jnp.sum(v, -1, keepdims=True) for v in values)
    mean = total / width
    centers = [v - mean for v in values]
    spread = sum(jnp.sum(c * c, -1, keepdims=True) for c in centers) / width
    return centers, lax.rsqrt(spread + EPS)


def norm_back(grads, centers, scale, width):
    normal = [c * scale for c in centers]
    mean_g = sum(jnp.sum(g, -1, keepdims=True) for g in grads) / width
    mean_gn = sum(jnp.sum(g * n, -1, keepdims=True) for g, n in zip(grads, normal)) / width
    return [scale * (g - mean_g - n * mean_gn) for g, n in zip(grads, normal)]


def segments():
    a = lax.broadcasted_iota(jnp.int32, (128, 128), 0) // 64
    b = lax.broadcasted_iota(jnp.int32, (128, 128), 1) // 64
    return jnp.where(a == b, 1.0, 0.0).astype(BF)


def head_sums(values, ones):
    high = values.astype(BF)
    low = (values - high.astype(F32)).astype(BF)
    return dot(high, ones) + dot(low, ones)


def by_head(v):
    lane = lax.broadcasted_iota(jnp.int32, v.shape, 1)
    zero = jnp.zeros_like(v)
    return jnp.concatenate([jnp.where(lane < 64, v, zero), jnp.where(lane < 64, zero, v)], 0)


def attend(q, k, scale_a, scale_b, split, ones):
    qf, kf = q.astype(F32), k.astype(F32)
    q_sum, k_sum = head_sums(qf * qf, ones), head_sums(kf * kf, ones)
    q_len = jnp.maximum(jnp.sqrt(q_sum), 1.0)
    k_len = jnp.maximum(jnp.sqrt(k_sum), 1.0)
    q_unit = (qf / q_len).astype(BF)
    k_unit = (kf / k_len).astype(BF)
    q_two = by_head(q_unit)
    row = lax.broadcasted_iota(jnp.int32, (256, 128), 0)
    col = lax.broadcasted_iota(jnp.int32, (256, 128), 1)
    scale = jnp.where(row < 128, scale_a, scale_b)
    raw = jnp.exp(dot(q_two, k_unit, 1, 1) * scale)
    apart = jnp.bitwise_and(lax.shift_right_logical(jnp.bitwise_xor(row, col), 2), 1)
    raw = jnp.where(apart * split == 0, raw, 0.0)
    soft = raw / jnp.sum(raw, -1, keepdims=True)
    return q_sum, k_sum, q_len, k_len, q_two, k_unit, scale, soft


def load_out_weights(w_ref, wo_ref):
    for m in range(4):
        for j in range(4):
            wo_ref[m * 128 : m * 128 + 128, j * 128 : j * 128 + 128] = w_ref[
                m, j * 128 : j * 128 + 128, 384:512
            ]


def forward_body(who, scales, x_ref, w_ref, hid_ref, mrg_ref, stk_ref, wo_ref, mix_ref):
    split = jnp.where(jnp.logical_and(who[1] == who[3] - 1, who[0] >= 2), 1, 0)
    load_out_weights(w_ref, wo_ref)
    ones = segments()
    x = x_ref[...].astype(F32)
    (center,), scale = norm_parts([x], 512)
    normed = (center * scale).astype(BF)
    for p in range(4):
        stacked = dot(normed, w_ref[p, :, 0:384]).astype(BF)
        stk_ref[p] = stacked
        soft = attend(
            stacked[:, 0:128],
            stacked[:, 128:256],
            scales[2 * p],
            scales[2 * p + 1],
            split,
            ones,
        )[-1].astype(BF)
        values = by_head(stacked[:, 256:384])
        both = jnp.concatenate([soft[0:128], soft[128:256]], 1)
        mix_ref[:, p * 128 : p * 128 + 128] = dot(both, values).astype(BF)
    hidden = (x + dot(mix_ref[...], wo_ref[...])).astype(BF)
    hid_ref[...] = hidden
    parts = [hidden[i * 32 : i * 32 + 32].astype(F32) for i in range(4)]
    centers, scale = norm_parts(parts, 2048)
    for i in range(4):
        piece = (centers[i] * scale).astype(BF)
        for d in range(4):
            mrg_ref[d, :, i * 512 : i * 512 + 512] = piece


def backward_body(who, scales, x_ref, dh_ref, stk_ref, w_ref, out_ref, wo_ref, acc_ref):
    split = jnp.where(jnp.logical_and(who[1] == who[3] - 1, who[0] >= 2), 1, 0)
    load_out_weights(w_ref, wo_ref)
    ones = segments()
    dh = dh_ref[...]
    for p in range(4):
        stacked = stk_ref[p]
        q, k, v = stacked[:, 0:128], stacked[:, 128:256], stacked[:, 256:384]
        d_mix = dot(dh, wo_ref[p * 128 : p * 128 + 128, :], 1, 1).astype(BF)
        q_sum, k_sum, q_len, k_len, q_two, k_unit, scale, soft = attend(
            q, k, scales[2 * p], scales[2 * p + 1], split, ones
        )
        d_two = by_head(d_mix)
        d_soft = dot(d_two, v, 1, 1).astype(BF).astype(F32)
        d_v = dot(soft.astype(BF), d_two, 0, 0).astype(BF)
        inner = jnp.sum(d_soft * soft, -1, keepdims=True)
        d_score = (soft * (d_soft - inner) * scale).astype(BF)
        both = jnp.concatenate([d_score[0:128], d_score[128:256]], 1)
        d_q = dot(both, by_head(k_unit)).astype(BF).astype(F32)
        d_k = dot(d_score, q_two, 0, 0).astype(BF).astype(F32)

        def unit_back(raw, grad, total, length):
            values = raw.astype(F32)
            share = jnp.where(total > 1.0, 1.0, jnp.where(total == 1.0, 0.5, 0.0))
            along = head_sums(values * grad, ones) * share / jnp.maximum(total, 1.0)
            return ((grad - values * along) / length).astype(BF)

        d_stack = jnp.concatenate(
            [unit_back(q, d_q, q_sum, q_len), unit_back(k, d_k, k_sum, k_len), d_v], 1
        )
        part = dot(d_stack, w_ref[p, :, 0:384], 1, 1)
        if p == 0:
            acc_ref[...] = part
        else:
            acc_ref[...] += part
    d_normed = acc_ref[...].astype(BF).astype(F32)
    (center,), scale = norm_parts([x_ref[...].astype(F32)], 512)
    (d_x,) = norm_back([d_normed], [center], scale, 512)
    grad = (dh.astype(F32) + d_x.astype(BF).astype(F32)).astype(BF)
    send_strips(grad, who[0], out_ref, 0)


def send_strips(window, me, out_ref, at):
    half = jnp.bitwise_and(me, 1)
    for m in range(4):
        strip = (m + 3) % 4
        mine = (half == strip // 2).astype(F32).astype(BF)
        for ab in range(4):
            row = ab * 32 + (strip % 2) * 16
            out_ref[m, at + ab * 16 : at + ab * 16 + 16, :] = window[row : row + 16] * mine


def first_weights_body(who, own_ref, other_ref, dexp_ref, mrg_ref, exp_ref, out_ref):
    core = who[2]
    for ref, c in ((own_ref, core), (other_ref, 1 - core)):
        for x in range(4):
            for z in range(2):
                for la in range(4):
                    mrg_ref[x, z, c, la * 32 : la * 32 + 32, :] = ref[x, la, z]
                for la in range(4, 8):
                    r = (la % 2) * 32
                    n = ((la - 4) // 2) * 256
                    exp_ref[x, z, c, r : r + 32, n : n + 256] = ref[x, la, z]
    blocks = []
    for ih in range(2):
        for strip in range(4):
            blocks.append(dexp_ref[(strip + 1) % 4, ih * 16 : ih * 16 + 16, :])
    d_exp = jnp.concatenate(blocks, 0)
    part = dot(d_exp, exp_ref[...].reshape(1024, 512), 1, 1).astype(BF)
    for d in range(4):
        out_ref[d] = part


def merge_body(in_ref, w_ref, out_ref):
    part = dot(in_ref[...].reshape(128, 2048), w_ref[...]).astype(BF)
    for d in range(4):
        out_ref[d] = part


def dense_body(
    who, own_ref, other_ref, coarse_ref, dco_ref, out_ref, crs_ref, dout_ref, w1_ref, w2_ref
):
    core = who[2]
    for ref, c in ((own_ref, core), (other_ref, 1 - core)):
        for x in range(4):
            for z in range(2):
                for j in range(4):
                    w1_ref[x, z, c, :, j * 256 : j * 256 + 256] = ref[x, j, z]
                    w2_ref[x, z, c, :, j * 256 : j * 256 + 256] = ref[x, j + 4, z]
    w1 = w1_ref[...].reshape(1024, 1024)
    w2 = w2_ref[...].reshape(1024, 1024)
    parts = [coarse_ref[j].astype(F32) for j in range(4)]
    centers, scale = norm_parts(parts, 1024)
    for j in range(4):
        crs_ref[:, j * 256 : j * 256 + 256] = coarse_ref[j]
    normed = jnp.concatenate([(c * scale).astype(BF) for c in centers], 1)
    d_out = (
        dco_ref[0].astype(F32)
        + dco_ref[1].astype(F32)
        + dco_ref[2].astype(F32)
        + dco_ref[3].astype(F32)
    ).astype(BF)
    dout_ref[...] = d_out
    inner = dot(normed, w1).astype(BF).astype(F32)
    d_act = dot(d_out, w2).astype(BF).astype(F32)
    rate = 0.7978845608028654
    t = jnp.tanh(rate * (inner + 0.044715 * (inner * inner * inner)))
    share = 0.5 * (1.0 + t)
    act = (inner * share).astype(BF)
    slope = share + 0.5 * inner * (1.0 - t * t) * rate * (1.0 + 0.134145 * (inner * inner))
    d_inner = (d_act * slope).astype(BF)
    d_norm = dot(d_inner, w1, 1, 1).astype(BF)
    outer = dot(act, w2, 1, 1).astype(BF)
    for d in range(4):
        out_ref[d, 0:128] = d_norm
        out_ref[d, 128:160] = outer[d * 32 : d * 32 + 32]


def coarse_back_body(who, recv_ref, crs_ref, dout_ref, w_ref, out_ref, cols_ref):
    me = who[0]
    coarse = crs_ref[...].astype(F32)
    d_norm = (
        recv_ref[0, 0:128].astype(F32)
        + recv_ref[1, 0:128].astype(F32)
        + recv_ref[2, 0:128].astype(F32)
        + recv_ref[3, 0:128].astype(F32)
    )
    d_norm = d_norm.astype(BF).astype(F32)
    (center,), scale = norm_parts([coarse], 1024)
    (d_c,) = norm_back([d_norm], [center], scale, 1024)
    d_coarse = (dout_ref[...].astype(F32) + d_c.astype(BF).astype(F32)).astype(BF)
    for j in range(4):
        cols_ref[j] = d_coarse[:, j * 256 : j * 256 + 256]
    part = dot(cols_ref[me], w_ref[...], 1, 1).astype(BF)
    own = crs_ref[pl.ds(pl.multiple_of(me * 32, 32), 32), :].astype(F32)
    outer = (
        recv_ref[0, 128:160].astype(F32)
        + recv_ref[1, 128:160].astype(F32)
        + recv_ref[2, 128:160].astype(F32)
        + recv_ref[3, 128:160].astype(F32)
    )
    coarse_out = (own + outer).astype(BF)
    for d in range(4):
        out_ref[d, :, 0:2048] = part[d * 32 : d * 32 + 32]
        out_ref[d, :, 2048:3072] = coarse_out


def hidden_back_body(who, recv_ref, hid_ref, g_ref, out_ref):
    half = jnp.bitwise_and(who[0], 1)
    first, second = 2 * half + 1, jnp.bitwise_and(2 * half + 2, 3)
    parts, grads = [], []
    for ab in range(4):
        lanes = slice(ab * 512, ab * 512 + 512)
        total = (
            recv_ref[0, :, lanes].astype(F32)
            + recv_ref[1, :, lanes].astype(F32)
            + recv_ref[2, :, lanes].astype(F32)
            + recv_ref[3, :, lanes].astype(F32)
        )
        grads.append(total.astype(BF).astype(F32))
        parts.append(hid_ref[ab * 32 : ab * 32 + 32].astype(F32))
    centers, scale = norm_parts(parts, 2048)
    back = norm_back(grads, centers, scale, 2048)
    for ab in range(4):
        for sp, source in ((0, first), (1, second)):
            rows = slice(ab * 32 + sp * 16, ab * 32 + sp * 16 + 16)
            g = g_ref[source, 32 + ab * 16 : 32 + ab * 16 + 16, :].astype(F32)
            b = back[ab][sp * 16 : sp * 16 + 16].astype(BF).astype(F32)
            out_ref[rows, :] = (g + b).astype(BF)


def expand_body(who, recv_ref, hid_ref, w_ref, out_ref):
    coarse_out = recv_ref[:, :, 2048:3072].reshape(128, 1024)
    expanded = dot(coarse_out, w_ref[...]).astype(BF)
    for m in range(4):
        strip = (m + 3) % 4
        for ih in range(2):
            row = (ih * 2 + strip // 2) * 32 + (strip % 2) * 16
            out_ref[m, ih * 16 : ih * 16 + 16, :] = expanded[row : row + 16]
    send_strips(hid_ref[...], who[0], out_ref, 32)


def output_body(who, recv_ref, out_ref):
    half = lax.shift_right_logical(jnp.bitwise_and(who[0] + 3, 3), 1)
    for ih in range(2):
        for ab in range(4):
            hidden = recv_ref[ih * 2 + half, 32 + ab * 16 : 32 + ab * 16 + 16, :]
            added = recv_ref[ab, ih * 16 : ih * 16 + 16, :]
            row = (ih * 4 + ab) * 16
            out_ref[row : row + 16, :] = (hidden.astype(F32) + added.astype(F32)).astype(BF)


def pick(index, source):
    chosen = index[:, None] == jnp.arange(source.shape[0], dtype=jnp.int32)[None]
    return jnp.dot(chosen.astype(BF), source, preferred_element_type=F32).astype(BF)


def grid_of(*sizes):
    return [a.reshape(-1) for a in np.indices(sizes, dtype=np.int32)]


def per_device(x, qk, wv, wo, scales, w_merge, w_first, w_second, w_expand, g):
    lat = lax.axis_index("lat")
    lats = lax.axis_size("lat")
    core = lax.axis_index("core")
    me = lax.axis_index("mp")
    lons = lax.axis_size(LON)
    who = jnp.stack([me, lat, core, lats]).astype(jnp.int32)

    x_flat = x.reshape(512, 512)
    g_flat = g.reshape(128, 512)
    rows = jnp.concatenate(
        [x_flat[0:64], x_flat[256:320], g_flat[0:16], g_flat[64:80]], 0
    )
    rows = lax.ppermute(rows, "lat", [(i, (i - 1) % lats) for i in range(lats)])
    source = jnp.concatenate([x_flat, rows[0:128], g_flat, rows[128:160]], 0)
    ih, a, b, lv, i4, j2 = grid_of(2, 2, 2, 2, 4, 2)
    r, c = ih * 8 + i4 * 2 + a, j2 * 2 + b
    from_g = np.where(r < 12, 640 + lv * 64 + (r + 4) * 4 + c, 768 + lv * 16 + (r - 12) * 4 + c)
    from_x = np.where(r < 12, lv * 256 + (r + 4) * 16 + c, 512 + lv * 64 + (r - 12) * 16 + c)
    sent = pick(jnp.where(me == 0, from_g, from_x), source)
    came = lax.ppermute(sent, LON, [(i, (i - 1) % lons) for i in range(lons)])
    g_strip = jnp.where(me == 0, came, pick(jnp.asarray(from_g), source))
    a, b, sp, lv, i4, j2 = grid_of(2, 2, 2, 2, 4, 2)
    r = (me // 2) * 8 + i4 * 2 + a
    c = 4 + (me % 2) * 8 + sp * 4 + j2 * 2 + b
    near = jnp.where(r < 12, lv * 256 + (r + 4) * 16 + c, 512 + lv * 64 + (r - 12) * 16 + c)
    far = 640 + (me // 2) * 64 + (a * 2 + b) * 16 + lv * 8 + i4 * 2 + j2
    x_win = pick(
        jnp.where(c < 16, near, far), jnp.concatenate([x_flat, rows[0:128], came], 0)
    )

    strip = g_strip.reshape(2, 4, 16, 512)
    blocks = []
    for d in range(4):
        fits = (d % 2) == ((me + 3) % 4) // 2
        blocks.append(
            jnp.concatenate(
                [
                    strip[:, d].reshape(32, 512),
                    jnp.where(fits, strip[d // 2].reshape(64, 512), jnp.zeros((), BF)),
                ],
                0,
            )
        )
    g_parts = swap(jnp.stack(blocks), "mp")

    wo_rows = jnp.concatenate([wo[:, j * 128 : j * 128 + 128] for j in range(4)], 0)
    qkvo = to_all(
        jnp.concatenate([qk[:, 0], qk[:, 1], wv, wo_rows], 1), "mp"
    )

    def gathered(shard):
        n = shard.shape[0] // lats
        piece = lax.dynamic_slice_in_dim(shard, lat * n, n, 0)
        own = to_all(to_all(piece, ("lat", "zh")).reshape(lats, 2, n, 256), "x").reshape(
            4, lats, 2, n, 256
        )
        return own, lax.ppermute(own, "core", [(0, 1), (1, 0)])

    one_own, one_other = gathered(
        jnp.concatenate([w_merge, w_expand[:, 0:256], w_expand[:, 256:512]], 0)
    )
    second = w_second.T
    two_own, two_other = gathered(
        jnp.concatenate(
            [w[:, j * 256 : j * 256 + 256] for w in (w_first, second) for j in range(4)], 0
        )
    )

    merge_full, expand_full, d_out_parts = call(
        first_weights_body,
        [arr(4, 2, 2, 128, 256), arr(4, 2, 2, 64, 512), arr(4, 128, 1024)],
        n_scalar=1,
        n_in=3,
    )(who, one_own, one_other, g_parts)
    merge_full = merge_full.reshape(2048, 256)
    expand_full = expand_full.reshape(1024, 512)
    d_out_parts = swap(d_out_parts, "mp")

    hidden, merged, stacked = call(
        forward_body,
        [arr(128, 512), arr(4, 32, 2048), arr(4, 128, 384)],
        [pltpu.VMEM((512, 512), BF), pltpu.VMEM((128, 512), BF)],
        n_scalar=2,
        n_in=2,
    )(who, scales, x_win, qkvo)
    merged = swap(merged, "mp")
    columns = call(merge_body, arr(4, 128, 256), n_in=2)(merged, merge_full)
    columns = swap(columns, "mp")
    sums, coarse, d_out = call(
        dense_body,
        [arr(4, 160, 1024), arr(128, 1024), arr(128, 1024)],
        [pltpu.VMEM((4, 2, 2, 64, 1024), BF), pltpu.VMEM((4, 2, 2, 64, 1024), BF)],
        n_scalar=1,
        n_in=4,
    )(who, two_own, two_other, columns, d_out_parts)
    sums = swap(sums, "mp")
    merges = call(
        coarse_back_body,
        arr(4, 32, 3072),
        [pltpu.VMEM((4, 128, 256), BF)],
        n_scalar=1,
        n_in=4,
    )(who, sums, coarse, d_out, merge_full)
    merges = swap(merges, "mp")
    d_hidden = call(hidden_back_body, arr(128, 512), n_scalar=1, n_in=3)(
        who, merges, hidden, g_parts
    )
    grads = call(
        backward_body,
        arr(4, 64, 512),
        [pltpu.VMEM((512, 512), BF), pltpu.VMEM((128, 512), F32)],
        n_scalar=2,
        n_in=4,
    )(who, scales, x_win, d_hidden, stacked, qkvo)
    grads = swap(grads, "mp")
    added = call(expand_body, arr(4, 96, 512), n_scalar=1, n_in=3)(
        who, merges, hidden, expand_full
    )
    added = swap(added, "mp")
    out_strip = call(output_body, arr(128, 512), n_scalar=1, n_in=1)(who, added)
    half = ((me + 3) % 4) // 2
    grad_strip = jnp.concatenate(
        [
            lax.dynamic_index_in_dim(grads, half, 0, False),
            lax.dynamic_index_in_dim(grads, half + 2, 0, False),
        ],
        0,
    )

    across = [(lon * 4, ((lon + 1) % lons) * 4) for lon in range(lons)]
    down = [
        ((la * lons + lon) * 4 + m, (((la + 1) % lats) * lons + (lon + (m == 0)) % lons) * 4 + m)
        for la in range(lats)
        for lon in range(lons)
        for m in range(4)
    ]
    lv, r, c = grid_of(2, 16, 4)
    s = r - 4
    kept = (s // 8) * 64 + ((s % 2) * 2 + c % 2) * 16 + lv * 8 + ((s % 8) // 2) * 2 + c // 2
    tops = np.where(
        r < 4, 256 + ((r % 2) * 2 + c % 2) * 8 + lv * 4 + (r // 2) * 2 + c // 2, 0
    )

    def rolled_back(strip):
        beyond = lax.ppermute(strip, LONMP, across)
        last = strip[64:128].reshape(8, 8, 512)[:, 4:8].reshape(32, 512)
        above = lax.ppermute(last, ALL, down)
        shift = jnp.where(me == 0, 128, 0)
        index = jnp.where(r < 4, tops, kept + shift)
        whole = pick(index, jnp.concatenate([strip, beyond, above], 0))
        return whole.reshape(2, 16, 4, 512)

    return rolled_back(out_strip), rolled_back(grad_strip)


def solution(mesh):
    lats, lons, mps = (mesh.shape[n] for n in ("lat", "lon", "mp"))
    fine = Mesh(
        mesh.devices.reshape(lats, lons // 4, 2, 2, mps), ("lat", "x", "zh", "core", "mp")
    )
    in_specs = (
        P(None, "lat", LON, None),
        P(None, None, "mp"),
        P(None, "mp"),
        P("mp", None),
        P(),
        P(LON, "mp"),
        P(LON, "mp"),
        P("mp", LON),
        P(LON, "mp"),
        P(None, "lat", LONMP, None),
    )
    out_specs = (P(None, "lat", LONMP, None), P(None, "lat", LONMP, None))
    return jax.shard_map(
        per_device, mesh=fine, in_specs=in_specs, out_specs=out_specs, check_vma=False
    )
```

```python
import jax
import jax.numpy as jnp
import numpy as np
from jax import lax
from jax.experimental import pallas as pl
from jax.experimental.pallas import tpu as pltpu
from jax.sharding import Mesh, PartitionSpec as P

BF, F32 = jnp.bfloat16, jnp.float32
EPS = 1e-05
LON = ("x", "zh", "core")
LONMP = LON + ("mp",)
ALL = ("lat",) + LONMP
STEPS = (0, 1, 3, 2)


def dot(a, b, ca=1, cb=0):
    return lax.dot_general(a, b, (((ca,), (cb,)), ((), ())), preferred_element_type=F32)


def to_all(value, axis):
    n = lax.axis_size(axis)
    return lax.all_to_all(
        jnp.broadcast_to(value[None], (n, *value.shape)), axis, 0, 0, tiled=True
    )


def swap(value, axis):
    return lax.all_to_all(value, axis, 0, 0, tiled=True)


def call(body, outs, scratch=(), n_scalar=0, n_in=0):
    specs = [pl.BlockSpec(memory_space=pltpu.SMEM)] * n_scalar + [
        pl.BlockSpec(memory_space=pltpu.VMEM)
    ] * n_in
    many = isinstance(outs, (list, tuple))
    ospecs = [pl.BlockSpec(memory_space=pltpu.VMEM)] * (len(outs) if many else 1)
    return pl.pallas_call(
        body,
        out_shape=outs,
        in_specs=specs,
        out_specs=ospecs if many else ospecs[0],
        scratch_shapes=list(scratch),
        compiler_params=pltpu.CompilerParams(vmem_limit_bytes=24 << 20),
    )


def arr(*shape, dtype=BF):
    return jax.ShapeDtypeStruct(shape, dtype)


def norm_parts(values, width):
    total = sum(jnp.sum(v, -1, keepdims=True) for v in values)
    mean = total / width
    centers = [v - mean for v in values]
    spread = sum(jnp.sum(c * c, -1, keepdims=True) for c in centers) / width
    return centers, lax.rsqrt(spread + EPS)


def norm_back(grads, centers, scale, width):
    normal = [c * scale for c in centers]
    mean_g = sum(jnp.sum(g, -1, keepdims=True) for g in grads) / width
    mean_gn = sum(jnp.sum(g * n, -1, keepdims=True) for g, n in zip(grads, normal)) / width
    return [scale * (g - mean_g - n * mean_gn) for g, n in zip(grads, normal)]


def segments():
    a = lax.broadcasted_iota(jnp.int32, (128, 128), 0) // 64
    b = lax.broadcasted_iota(jnp.int32, (128, 128), 1) // 64
    return jnp.where(a == b, 1.0, 0.0).astype(BF)


def head_sums(values, ones):
    high = values.astype(BF)
    low = (values - high.astype(F32)).astype(BF)
    return dot(high, ones) + dot(low, ones)


def by_head(v):
    lane = lax.broadcasted_iota(jnp.int32, v.shape, 1)
    zero = jnp.zeros_like(v)
    return jnp.concatenate([jnp.where(lane < 64, v, zero), jnp.where(lane < 64, zero, v)], 0)


def attend(q, k, scale_a, scale_b, split, ones):
    qf, kf = q.astype(F32), k.astype(F32)
    q_sum, k_sum = head_sums(qf * qf, ones), head_sums(kf * kf, ones)
    q_len = jnp.maximum(jnp.sqrt(q_sum), 1.0)
    k_len = jnp.maximum(jnp.sqrt(k_sum), 1.0)
    q_unit = (qf / q_len).astype(BF)
    k_unit = (kf / k_len).astype(BF)
    q_two = by_head(q_unit)
    row = lax.broadcasted_iota(jnp.int32, (256, 128), 0)
    col = lax.broadcasted_iota(jnp.int32, (256, 128), 1)
    scale = jnp.where(row < 128, scale_a, scale_b)
    raw = jnp.exp(dot(q_two, k_unit, 1, 1) * scale)
    apart = jnp.bitwise_and(lax.shift_right_logical(jnp.bitwise_xor(row, col), 2), 1)
    raw = jnp.where(apart * split == 0, raw, 0.0)
    soft = raw / jnp.sum(raw, -1, keepdims=True)
    return q_sum, k_sum, q_len, k_len, q_two, k_unit, scale, soft


def load_out_weights(w_ref, wo_ref):
    for m in range(4):
        for j in range(4):
            wo_ref[m * 128 : m * 128 + 128, j * 128 : j * 128 + 128] = w_ref[
                m, j * 128 : j * 128 + 128, 384:512
            ]


def forward_body(who, scales, x_ref, w_ref, g_ref, hid_ref, mrg_ref, stk_ref, wo_ref, mix_ref):
    split = jnp.where(jnp.logical_and(who[1] == who[3] - 1, who[0] >= 2), 1, 0)
    load_out_weights(w_ref, wo_ref)
    ones = segments()
    x = x_ref[...].astype(F32)
    (center,), scale = norm_parts([x], 512)
    normed = (center * scale).astype(BF)
    for p in range(4):
        stacked = dot(normed, w_ref[p, :, 0:384]).astype(BF)
        stk_ref[p] = stacked
        soft = attend(
            stacked[:, 0:128],
            stacked[:, 128:256],
            scales[2 * p],
            scales[2 * p + 1],
            split,
            ones,
        )[-1].astype(BF)
        values = by_head(stacked[:, 256:384])
        both = jnp.concatenate([soft[0:128], soft[128:256]], 1)
        mix_ref[:, p * 128 : p * 128 + 128] = dot(both, values).astype(BF)
    hidden = (x + dot(mix_ref[...], wo_ref[...])).astype(BF)
    hid_ref[...] = hidden
    parts = [hidden[i * 32 : i * 32 + 32].astype(F32) for i in range(4)]
    centers, scale = norm_parts(parts, 2048)
    for i in range(4):
        piece = (centers[i] * scale).astype(BF)
        for d in range(4):
            mrg_ref[d, 0:32, i * 512 : i * 512 + 512] = piece
    side = lax.shift_right_logical(jnp.bitwise_and(who[0] + 3, 3), 1)
    for d in range(4):
        for j in range(4):
            row = (j // 2) * 64 + d * 16 + (j % 2) * 8
            mrg_ref[d, 32:40, j * 512 : j * 512 + 512] = g_ref[row : row + 8]
            fits = (side == d % 2).astype(F32).astype(BF)
            row = (d // 2) * 64 + j * 16
            mrg_ref[d, 40:56, j * 512 : j * 512 + 512] = g_ref[row : row + 16] * fits


def backward_body(who, scales, x_ref, dh_ref, stk_ref, w_ref, out_ref, wo_ref, acc_ref):
    split = jnp.where(jnp.logical_and(who[1] == who[3] - 1, who[0] >= 2), 1, 0)
    load_out_weights(w_ref, wo_ref)
    ones = segments()
    dh = dh_ref[...]
    for p in range(4):
        stacked = stk_ref[p]
        q, k, v = stacked[:, 0:128], stacked[:, 128:256], stacked[:, 256:384]
        d_mix = dot(dh, wo_ref[p * 128 : p * 128 + 128, :], 1, 1).astype(BF)
        q_sum, k_sum, q_len, k_len, q_two, k_unit, scale, soft = attend(
            q, k, scales[2 * p], scales[2 * p + 1], split, ones
        )
        d_two = by_head(d_mix)
        d_soft = dot(d_two, v, 1, 1).astype(BF).astype(F32)
        d_v = dot(soft.astype(BF), d_two, 0, 0).astype(BF)
        inner = jnp.sum(d_soft * soft, -1, keepdims=True)
        d_score = (soft * (d_soft - inner) * scale).astype(BF)
        both = jnp.concatenate([d_score[0:128], d_score[128:256]], 1)
        d_q = dot(both, by_head(k_unit)).astype(BF).astype(F32)
        d_k = dot(d_score, q_two, 0, 0).astype(BF).astype(F32)

        def unit_back(raw, grad, total, length):
            values = raw.astype(F32)
            share = jnp.where(total > 1.0, 1.0, jnp.where(total == 1.0, 0.5, 0.0))
            along = head_sums(values * grad, ones) * share / jnp.maximum(total, 1.0)
            return ((grad - values * along) / length).astype(BF)

        d_stack = jnp.concatenate(
            [unit_back(q, d_q, q_sum, q_len), unit_back(k, d_k, k_sum, k_len), d_v], 1
        )
        part = dot(d_stack, w_ref[p, :, 0:384], 1, 1)
        if p == 0:
            acc_ref[...] = part
        else:
            acc_ref[...] += part
    d_normed = acc_ref[...].astype(BF).astype(F32)
    (center,), scale = norm_parts([x_ref[...].astype(F32)], 512)
    (d_x,) = norm_back([d_normed], [center], scale, 512)
    grad = (dh.astype(F32) + d_x.astype(BF).astype(F32)).astype(BF)
    send_strips(grad, who[0], out_ref, 0)


def send_strips(window, me, out_ref, at):
    half = jnp.bitwise_and(me, 1)
    for m in range(4):
        strip = (m + 3) % 4
        mine = (half == strip // 2).astype(F32).astype(BF)
        for ab in range(4):
            row = ab * 32 + (strip % 2) * 16
            out_ref[m, at + ab * 16 : at + ab * 16 + 16, :] = window[row : row + 16] * mine


def placed(who, refs):
    x, core = who[4], who[2]
    own, other = refs[0:4], refs[4]
    for step in range(4):
        yield own[step], jnp.bitwise_and(x - STEPS[step], 3), core
        yield other.at[step], jnp.bitwise_and(x - STEPS[step], 3), 1 - core


def merge_body(who, r0, r1, r2, r3, ro, in_ref, mrg_ref, exp_ref, out_ref):
    for ref, x, c in placed(who, (r0, r1, r2, r3, ro)):
        for z in range(2):
            for la in range(4):
                mrg_ref[x, z, c, la * 32 : la * 32 + 32, :] = ref[la, z]
            for la in range(4, 8):
                r = (la % 2) * 32
                n = ((la - 4) // 2) * 256
                exp_ref[x, z, c, r : r + 32, n : n + 256] = ref[la, z]
    blocks = []
    for ih in range(2):
        for strip in range(4):
            for j in range(2 * ih, 2 * ih + 2):
                blocks.append(in_ref[(strip + 1) % 4, 32:40, j * 512 : j * 512 + 512])
    d_exp = jnp.concatenate(blocks, 0)
    d_out = dot(d_exp, exp_ref[...].reshape(1024, 512), 1, 1).astype(BF)
    merged = in_ref[:, 0:32, :].reshape(128, 2048)
    columns = dot(merged, mrg_ref[...].reshape(2048, 256)).astype(BF)
    for d in range(4):
        out_ref[d, :, 0:256] = columns
        out_ref[d, :, 256:1280] = d_out


def dense_body(
    who, r0, r1, r2, r3, ro, in_ref, out_ref, crs_ref, dout_ref, w1_ref, w2_ref
):
    for ref, x, c in placed(who, (r0, r1, r2, r3, ro)):
        for z in range(2):
            for j in range(4):
                w1_ref[x, z, c, :, j * 256 : j * 256 + 256] = ref[j, z]
                w2_ref[x, z, c, :, j * 256 : j * 256 + 256] = ref[j + 4, z]
    w1 = w1_ref[...].reshape(1024, 1024)
    w2 = w2_ref[...].reshape(1024, 1024)
    parts = [in_ref[j, :, 0:256].astype(F32) for j in range(4)]
    centers, scale = norm_parts(parts, 1024)
    for j in range(4):
        crs_ref[:, j * 256 : j * 256 + 256] = in_ref[j, :, 0:256]
    normed = jnp.concatenate([(c * scale).astype(BF) for c in centers], 1)
    d_out = (
        in_ref[0, :, 256:1280].astype(F32)
        + in_ref[1, :, 256:1280].astype(F32)
        + in_ref[2, :, 256:1280].astype(F32)
        + in_ref[3, :, 256:1280].astype(F32)
    ).astype(BF)
    dout_ref[...] = d_out
    inner = dot(normed, w1).astype(BF).astype(F32)
    d_act = dot(d_out, w2).astype(BF).astype(F32)
    rate = 0.7978845608028654
    t = jnp.tanh(rate * (inner + 0.044715 * (inner * inner * inner)))
    share = 0.5 * (1.0 + t)
    act = (inner * share).astype(BF)
    slope = share + 0.5 * inner * (1.0 - t * t) * rate * (1.0 + 0.134145 * (inner * inner))
    d_inner = (d_act * slope).astype(BF)
    d_norm = dot(d_inner, w1, 1, 1).astype(BF)
    outer = dot(act, w2, 1, 1).astype(BF)
    for d in range(4):
        out_ref[d, 0:128] = d_norm
        out_ref[d, 128:160] = outer[d * 32 : d * 32 + 32]


def coarse_back_body(who, recv_ref, crs_ref, dout_ref, w_ref, out_ref, cols_ref):
    me = who[0]
    coarse = crs_ref[...].astype(F32)
    d_norm = (
        recv_ref[0, 0:128].astype(F32)
        + recv_ref[1, 0:128].astype(F32)
        + recv_ref[2, 0:128].astype(F32)
        + recv_ref[3, 0:128].astype(F32)
    )
    d_norm = d_norm.astype(BF).astype(F32)
    (center,), scale = norm_parts([coarse], 1024)
    (d_c,) = norm_back([d_norm], [center], scale, 1024)
    d_coarse = (dout_ref[...].astype(F32) + d_c.astype(BF).astype(F32)).astype(BF)
    for j in range(4):
        cols_ref[j] = d_coarse[:, j * 256 : j * 256 + 256]
    part = dot(cols_ref[me], w_ref[...], 1, 1).astype(BF)
    own = crs_ref[pl.ds(pl.multiple_of(me * 32, 32), 32), :].astype(F32)
    outer = (
        recv_ref[0, 128:160].astype(F32)
        + recv_ref[1, 128:160].astype(F32)
        + recv_ref[2, 128:160].astype(F32)
        + recv_ref[3, 128:160].astype(F32)
    )
    coarse_out = (own + outer).astype(BF)
    for d in range(4):
        out_ref[d, :, 0:2048] = part[d * 32 : d * 32 + 32]
        out_ref[d, :, 2048:3072] = coarse_out


def hidden_back_body(who, recv_ref, hid_ref, g_ref, out_ref):
    half = jnp.bitwise_and(who[0], 1)
    first, second = 2 * half + 1, jnp.bitwise_and(2 * half + 2, 3)
    parts, grads = [], []
    for ab in range(4):
        lanes = slice(ab * 512, ab * 512 + 512)
        total = (
            recv_ref[0, :, lanes].astype(F32)
            + recv_ref[1, :, lanes].astype(F32)
            + recv_ref[2, :, lanes].astype(F32)
            + recv_ref[3, :, lanes].astype(F32)
        )
        grads.append(total.astype(BF).astype(F32))
        parts.append(hid_ref[ab * 32 : ab * 32 + 32].astype(F32))
    centers, scale = norm_parts(parts, 2048)
    back = norm_back(grads, centers, scale, 2048)
    for ab in range(4):
        lanes = slice(ab * 512, ab * 512 + 512)
        for sp, source in ((0, first), (1, second)):
            rows = slice(ab * 32 + sp * 16, ab * 32 + sp * 16 + 16)
            g = g_ref[source, 40:56, lanes].astype(F32)
            b = back[ab][sp * 16 : sp * 16 + 16].astype(BF).astype(F32)
            out_ref[rows, :] = (g + b).astype(BF)


def expand_body(who, recv_ref, hid_ref, w_ref, out_ref):
    coarse_out = recv_ref[:, :, 2048:3072].reshape(128, 1024)
    expanded = dot(coarse_out, w_ref[...]).astype(BF)
    for m in range(4):
        strip = (m + 3) % 4
        for ih in range(2):
            row = (ih * 2 + strip // 2) * 32 + (strip % 2) * 16
            out_ref[m, ih * 16 : ih * 16 + 16, :] = expanded[row : row + 16]
    send_strips(hid_ref[...], who[0], out_ref, 32)


def output_body(who, recv_ref, out_ref):
    half = lax.shift_right_logical(jnp.bitwise_and(who[0] + 3, 3), 1)
    for ih in range(2):
        for ab in range(4):
            hidden = recv_ref[ih * 2 + half, 32 + ab * 16 : 32 + ab * 16 + 16, :]
            added = recv_ref[ab, ih * 16 : ih * 16 + 16, :]
            row = (ih * 4 + ab) * 16
            out_ref[row : row + 16, :] = (hidden.astype(F32) + added.astype(F32)).astype(BF)


def pick(index, source):
    chosen = index[:, None] == jnp.arange(source.shape[0], dtype=jnp.int32)[None]
    return jnp.dot(chosen.astype(BF), source, preferred_element_type=F32).astype(BF)


def grid_of(*sizes):
    return [a.reshape(-1) for a in np.indices(sizes, dtype=np.int32)]


def whole_step(x, qk, wv, wo, scales, w_merge, w_first, w_second, w_expand, g):
    lat = lax.axis_index("lat")
    lats = lax.axis_size("lat")
    core = lax.axis_index("core")
    me = lax.axis_index("mp")
    lons = lax.axis_size(LON)
    who = jnp.stack([me, lat, core, lats, lax.axis_index("x")]).astype(jnp.int32)

    x_flat = x.reshape(512, 512)
    g_flat = g.reshape(128, 512)
    rows = jnp.concatenate(
        [x_flat[0:64], x_flat[256:320], g_flat[0:16], g_flat[64:80]], 0
    )
    rows = lax.ppermute(rows, "lat", [(i, (i - 1) % lats) for i in range(lats)])
    source = jnp.concatenate([x_flat, rows[0:128], g_flat, rows[128:160]], 0)
    ih, a, b, lv, i4, j2 = grid_of(2, 2, 2, 2, 4, 2)
    r, c = ih * 8 + i4 * 2 + a, j2 * 2 + b
    from_g = np.where(r < 12, 640 + lv * 64 + (r + 4) * 4 + c, 768 + lv * 16 + (r - 12) * 4 + c)
    from_x = np.where(r < 12, lv * 256 + (r + 4) * 16 + c, 512 + lv * 64 + (r - 12) * 16 + c)
    sent = pick(jnp.where(me == 0, from_g, from_x), source)
    came = lax.ppermute(sent, LON, [(i, (i - 1) % lons) for i in range(lons)])
    g_strip = jnp.where(me == 0, came, pick(jnp.asarray(from_g), source))
    a, b, sp, lv, i4, j2 = grid_of(2, 2, 2, 2, 4, 2)
    r = (me // 2) * 8 + i4 * 2 + a
    c = 4 + (me % 2) * 8 + sp * 4 + j2 * 2 + b
    near = jnp.where(r < 12, lv * 256 + (r + 4) * 16 + c, 512 + lv * 64 + (r - 12) * 16 + c)
    far = 640 + (me // 2) * 64 + (a * 2 + b) * 16 + lv * 8 + i4 * 2 + j2
    x_win = pick(
        jnp.where(c < 16, near, far), jnp.concatenate([x_flat, rows[0:128], came], 0)
    )

    wo_rows = jnp.concatenate([wo[:, j * 128 : j * 128 + 128] for j in range(4)], 0)
    qkvo = to_all(jnp.concatenate([qk[:, 0], qk[:, 1], wv, wo_rows], 1), "mp")

    def piece(shard):
        n = shard.shape[0] // lats
        return lax.dynamic_slice_in_dim(shard, lat * n, n, 0)

    second = w_second.T
    one = jnp.concatenate([w_merge, w_expand[:, 0:256], w_expand[:, 256:512]], 0)
    two = jnp.concatenate(
        [w[:, j * 256 : j * 256 + 256] for w in (w_first, second) for j in range(4)], 0
    )
    shards = to_all(jnp.concatenate([piece(one), piece(two)], 0), ("lat", "zh"))
    shards = shards.reshape(lats, 2, 96, 256)

    def gathered(own):
        parts = [own]
        for step in STEPS[1:]:
            parts.append(lax.ppermute(own, "x", [(i, (i + step) % 4) for i in range(4)]))
        other = lax.ppermute(jnp.stack(parts), "core", [(0, 1), (1, 0)])
        return (*parts, other)

    one_parts = gathered(shards[:, :, 0:32])
    two_parts = gathered(shards[:, :, 32:96])

    hidden, merged, stacked = call(
        forward_body,
        [arr(128, 512), arr(4, 56, 2048), arr(4, 128, 384)],
        [pltpu.VMEM((512, 512), BF), pltpu.VMEM((128, 512), BF)],
        n_scalar=2,
        n_in=3,
    )(who, scales, x_win, qkvo, g_strip)
    merged = swap(merged, "mp")
    merge_full, expand_full, columns = call(
        merge_body,
        [arr(4, 2, 2, 128, 256), arr(4, 2, 2, 64, 512), arr(4, 128, 1280)],
        n_scalar=1,
        n_in=6,
    )(who, *one_parts, merged)
    merge_full = merge_full.reshape(2048, 256)
    expand_full = expand_full.reshape(1024, 512)
    columns = swap(columns, "mp")
    sums, coarse, d_out = call(
        dense_body,
        [arr(4, 160, 1024), arr(128, 1024), arr(128, 1024)],
        [pltpu.VMEM((4, 2, 2, 64, 1024), BF), pltpu.VMEM((4, 2, 2, 64, 1024), BF)],
        n_scalar=1,
        n_in=6,
    )(who, *two_parts, columns)
    sums = swap(sums, "mp")
    merges = call(
        coarse_back_body,
        arr(4, 32, 3072),
        [pltpu.VMEM((4, 128, 256), BF)],
        n_scalar=1,
        n_in=4,
    )(who, sums, coarse, d_out, merge_full)
    merges = swap(merges, "mp")
    d_hidden = call(hidden_back_body, arr(128, 512), n_scalar=1, n_in=3)(
        who, merges, hidden, merged
    )
    grads = call(
        backward_body,
        arr(4, 64, 512),
        [pltpu.VMEM((512, 512), BF), pltpu.VMEM((128, 512), F32)],
        n_scalar=2,
        n_in=4,
    )(who, scales, x_win, d_hidden, stacked, qkvo)
    grads = swap(grads, "mp")
    added = call(expand_body, arr(4, 96, 512), n_scalar=1, n_in=3)(
        who, merges, hidden, expand_full
    )
    added = swap(added, "mp")
    out_strip = call(output_body, arr(128, 512), n_scalar=1, n_in=1)(who, added)
    half = ((me + 3) % 4) // 2
    grad_strip = jnp.concatenate(
        [
            lax.dynamic_index_in_dim(grads, half, 0, False),
            lax.dynamic_index_in_dim(grads, half + 2, 0, False),
        ],
        0,
    )

    across = [(lon * 4, ((lon + 1) % lons) * 4) for lon in range(lons)]
    down = [
        ((la * lons + lon) * 4 + m, (((la + 1) % lats) * lons + (lon + (m == 0)) % lons) * 4 + m)
        for la in range(lats)
        for lon in range(lons)
        for m in range(4)
    ]
    lv, r, c = grid_of(2, 16, 4)
    s = r - 4
    kept = (s // 8) * 64 + ((s % 2) * 2 + c % 2) * 16 + lv * 8 + ((s % 8) // 2) * 2 + c // 2
    tops = np.where(
        r < 4, 256 + ((r % 2) * 2 + c % 2) * 8 + lv * 4 + (r // 2) * 2 + c // 2, 0
    )

    def rolled_back(strip):
        beyond = lax.ppermute(strip, LONMP, across)
        last = strip[64:128].reshape(8, 8, 512)[:, 4:8].reshape(32, 512)
        above = lax.ppermute(last, ALL, down)
        shift = jnp.where(me == 0, 128, 0)
        index = jnp.where(r < 4, tops, kept + shift)
        whole = pick(index, jnp.concatenate([strip, beyond, above], 0))
        return whole.reshape(2, 16, 4, 512)

    return rolled_back(out_strip), rolled_back(grad_strip)


def solution(mesh):
    lats, lons, mps = (mesh.shape[n] for n in ("lat", "lon", "mp"))
    fine = Mesh(
        mesh.devices.reshape(lats, lons // 4, 2, 2, mps), ("lat", "x", "zh", "core", "mp")
    )
    in_specs = (
        P(None, "lat", LON, None),
        P(None, None, "mp"),
        P(None, "mp"),
        P("mp", None),
        P(),
        P(LON, "mp"),
        P(LON, "mp"),
        P("mp", LON),
        P(LON, "mp"),
        P(None, "lat", LONMP, None),
    )
    out_specs = (P(None, "lat", LONMP, None), P(None, "lat", LONMP, None))
    return jax.shard_map(
        whole_step, mesh=fine, in_specs=in_specs, out_specs=out_specs, check_vma=False
    )
```

```python
import jax
import jax.numpy as jnp
import numpy as np
from jax import lax
from jax.experimental import pallas as pl
from jax.experimental.pallas import tpu as pltpu
from jax.sharding import Mesh, PartitionSpec as P

BF, F32 = jnp.bfloat16, jnp.float32
EPS = 1e-05
LON = ("x", "zh", "core")
LONMP = LON + ("mp",)
ALL = ("lat",) + LONMP
STEPS = (0, 1, 3, 2)


def dot(a, b, ca=1, cb=0):
    return lax.dot_general(a, b, (((ca,), (cb,)), ((), ())), preferred_element_type=F32)


def swap(value, axis):
    return lax.all_to_all(value, axis, 0, 0, tiled=True)


def call(body, outs, scratch=(), n_scalar=0, n_in=0):
    specs = [pl.BlockSpec(memory_space=pltpu.SMEM)] * n_scalar + [pl.BlockSpec()] * n_in
    many = isinstance(outs, (list, tuple))
    ospecs = [pl.BlockSpec()] * (len(outs) if many else 1)
    return pl.pallas_call(
        body,
        out_shape=outs,
        in_specs=specs,
        out_specs=ospecs if many else ospecs[0],
        scratch_shapes=list(scratch),
        compiler_params=pltpu.CompilerParams(vmem_limit_bytes=24 << 20),
    )


def arr(*shape, dtype=BF):
    return jax.ShapeDtypeStruct(shape, dtype)


def norm_parts(values, width):
    total = sum(jnp.sum(v, -1, keepdims=True) for v in values)
    mean = total / width
    centers = [v - mean for v in values]
    spread = sum(jnp.sum(c * c, -1, keepdims=True) for c in centers) / width
    return centers, lax.rsqrt(spread + EPS)


def norm_back(grads, centers, scale, width):
    normal = [c * scale for c in centers]
    mean_g = sum(jnp.sum(g, -1, keepdims=True) for g in grads) / width
    mean_gn = sum(jnp.sum(g * n, -1, keepdims=True) for g, n in zip(grads, normal)) / width
    return [scale * (g - mean_g - n * mean_gn) for g, n in zip(grads, normal)]


def segments():
    a = lax.broadcasted_iota(jnp.int32, (128, 128), 0) // 64
    b = lax.broadcasted_iota(jnp.int32, (128, 128), 1) // 64
    return jnp.where(a == b, 1.0, 0.0).astype(BF)


def head_sums(values, ones):
    high = values.astype(BF)
    low = (values - high.astype(F32)).astype(BF)
    return dot(high, ones) + dot(low, ones)


def by_head(v):
    lane = lax.broadcasted_iota(jnp.int32, v.shape, 1)
    zero = jnp.zeros_like(v)
    return jnp.concatenate([jnp.where(lane < 64, v, zero), jnp.where(lane < 64, zero, v)], 0)


def attend(q, k, scale_a, scale_b, split, ones):
    qf, kf = q.astype(F32), k.astype(F32)
    q_sum, k_sum = head_sums(qf * qf, ones), head_sums(kf * kf, ones)
    q_len = jnp.maximum(jnp.sqrt(q_sum), 1.0)
    k_len = jnp.maximum(jnp.sqrt(k_sum), 1.0)
    q_unit = (qf / q_len).astype(BF)
    k_unit = (kf / k_len).astype(BF)
    q_two = by_head(q_unit)
    row = lax.broadcasted_iota(jnp.int32, (256, 128), 0)
    col = lax.broadcasted_iota(jnp.int32, (256, 128), 1)
    scale = jnp.where(row < 128, scale_a, scale_b)
    raw = jnp.exp(dot(q_two, k_unit, 1, 1) * scale)
    apart = jnp.bitwise_and(lax.shift_right_logical(jnp.bitwise_xor(row, col), 2), 1)
    raw = jnp.where(apart * split == 0, raw, 0.0)
    soft = raw / jnp.sum(raw, -1, keepdims=True)
    return q_sum, k_sum, q_len, k_len, q_two, k_unit, scale, soft


def pieces_body(who, mrg_ref, w1_ref, w2_ref, exp_ref, out_ref):
    def put(rows, value):
        for d in range(16):
            out_ref[d, rows, :] = value

    for la in range(8):

        @pl.when(who[1] == la)
        def _(la=la):
            if la < 4:
                put(slice(0, 32), mrg_ref[la * 32 : la * 32 + 32, :])
                put(slice(32, 96), w1_ref[:, la * 256 : la * 256 + 256])
            else:
                r, n = (la % 2) * 32, ((la - 4) // 2) * 256
                put(slice(0, 32), exp_ref[r : r + 32, n : n + 256])
                k = (la - 4) * 256
                put(slice(32, 96), w2_ref[k : k + 256, :].astype(F32).T.astype(BF))


def pair_of(who, step):
    return jnp.bitwise_and(who[0] - STEPS[step], 3)


def load_out_weights(who, w_refs, wo_ref):
    for step, ref in enumerate(w_refs):
        for j in range(4):
            wo_ref[pair_of(who, step), :, j * 128 : j * 128 + 128] = ref[
                j * 128 : j * 128 + 128, 384:512
            ]


def forward_body(
    who, scales, x_ref, w0, w1, w2, w3, g_ref, hid_ref, mrg_ref, stk_ref, wo_ref, mix_ref
):
    split = jnp.where(jnp.logical_and(who[1] == who[3] - 1, who[0] >= 2), 1, 0)
    load_out_weights(who, (w0, w1, w2, w3), wo_ref)
    ones = segments()
    x = x_ref[...].astype(F32)
    (center,), scale = norm_parts([x], 512)
    normed = (center * scale).astype(BF)
    for step, ref in enumerate((w0, w1, w2, w3)):
        p = pair_of(who, step)
        stacked = dot(normed, ref[:, 0:384]).astype(BF)
        stk_ref[step] = stacked
        soft = attend(
            stacked[:, 0:128],
            stacked[:, 128:256],
            scales[2 * p],
            scales[2 * p + 1],
            split,
            ones,
        )[-1].astype(BF)
        values = by_head(stacked[:, 256:384])
        both = jnp.concatenate([soft[0:128], soft[128:256]], 1)
        mix_ref[p] = dot(both, values).astype(BF)
    mixed = jnp.concatenate([mix_ref[p] for p in range(4)], 1)
    hidden = (x + dot(mixed, wo_ref[...].reshape(512, 512))).astype(BF)
    hid_ref[...] = hidden
    parts = [hidden[i * 32 : i * 32 + 32].astype(F32) for i in range(4)]
    centers, scale = norm_parts(parts, 2048)
    for i in range(4):
        piece = (centers[i] * scale).astype(BF)
        for d in range(4):
            mrg_ref[d, 0:32, i * 512 : i * 512 + 512] = piece
    side = lax.shift_right_logical(jnp.bitwise_and(who[0] + 3, 3), 1)
    for d in range(4):
        for j in range(4):
            row = (j // 2) * 64 + d * 16 + (j % 2) * 8
            mrg_ref[d, 32:40, j * 512 : j * 512 + 512] = g_ref[row : row + 8]
            fits = (side == d % 2).astype(F32).astype(BF)
            row = (d // 2) * 64 + j * 16
            mrg_ref[d, 40:56, j * 512 : j * 512 + 512] = g_ref[row : row + 16] * fits


def backward_body(
    who, scales, x_ref, dh_ref, stk_ref, w0, w1, w2, w3, out_ref, wo_ref, acc_ref
):
    split = jnp.where(jnp.logical_and(who[1] == who[3] - 1, who[0] >= 2), 1, 0)
    load_out_weights(who, (w0, w1, w2, w3), wo_ref)
    ones = segments()
    dh = dh_ref[...]
    for step, ref in enumerate((w0, w1, w2, w3)):
        p = pair_of(who, step)
        stacked = stk_ref[step]
        q, k, v = stacked[:, 0:128], stacked[:, 128:256], stacked[:, 256:384]
        d_mix = dot(dh, wo_ref[p], 1, 1).astype(BF)
        q_sum, k_sum, q_len, k_len, q_two, k_unit, scale, soft = attend(
            q, k, scales[2 * p], scales[2 * p + 1], split, ones
        )
        d_two = by_head(d_mix)
        d_soft = dot(d_two, v, 1, 1).astype(BF).astype(F32)
        d_v = dot(soft.astype(BF), d_two, 0, 0).astype(BF)
        inner = jnp.sum(d_soft * soft, -1, keepdims=True)
        d_score = (soft * (d_soft - inner) * scale).astype(BF)
        both = jnp.concatenate([d_score[0:128], d_score[128:256]], 1)
        d_q = dot(both, by_head(k_unit)).astype(BF).astype(F32)
        d_k = dot(d_score, q_two, 0, 0).astype(BF).astype(F32)

        def unit_back(raw, grad, total, length):
            values = raw.astype(F32)
            share = jnp.where(total > 1.0, 1.0, jnp.where(total == 1.0, 0.5, 0.0))
            along = head_sums(values * grad, ones) * share / jnp.maximum(total, 1.0)
            return ((grad - values * along) / length).astype(BF)

        d_stack = jnp.concatenate(
            [unit_back(q, d_q, q_sum, q_len), unit_back(k, d_k, k_sum, k_len), d_v], 1
        )
        part = dot(d_stack, ref[:, 0:384], 1, 1)
        if step == 0:
            acc_ref[...] = part
        else:
            acc_ref[...] += part
    d_normed = acc_ref[...].astype(BF).astype(F32)
    (center,), scale = norm_parts([x_ref[...].astype(F32)], 512)
    (d_x,) = norm_back([d_normed], [center], scale, 512)
    grad = (dh.astype(F32) + d_x.astype(BF).astype(F32)).astype(BF)
    send_strips(grad, who[0], out_ref, 0)


def send_strips(window, me, out_ref, at):
    half = jnp.bitwise_and(me, 1)
    for m in range(4):
        strip = (m + 3) % 4
        mine = (half == strip // 2).astype(F32).astype(BF)
        for ab in range(4):
            row = ab * 32 + (strip % 2) * 16
            out_ref[m, at + ab * 16 : at + ab * 16 + 16, :] = window[row : row + 16] * mine


def placed(who, refs):
    x, core = who[4], who[2]
    for step in range(4):
        yield refs[2 * step], jnp.bitwise_and(x - STEPS[step], 3), core
        yield refs[2 * step + 1], jnp.bitwise_and(x - STEPS[step], 3), 1 - core


def merge_body(who, *refs):
    in_ref, mrg_ref, exp_ref, out_ref = refs[8:]
    for ref, x, c in placed(who, refs):
        for z in range(2):
            for la in range(4):
                mrg_ref[x, z, c, la * 32 : la * 32 + 32, :] = ref[la, z]
            for la in range(4, 8):
                r = (la % 2) * 32
                n = ((la - 4) // 2) * 256
                exp_ref[x, z, c, r : r + 32, n : n + 256] = ref[la, z]
    blocks = []
    for ih in range(2):
        for strip in range(4):
            for j in range(2 * ih, 2 * ih + 2):
                blocks.append(in_ref[(strip + 1) % 4, 32:40, j * 512 : j * 512 + 512])
    d_exp = jnp.concatenate(blocks, 0)
    d_out = dot(d_exp, exp_ref[...].reshape(1024, 512), 1, 1).astype(BF)
    merged = in_ref[:, 0:32, :].reshape(128, 2048)
    columns = dot(merged, mrg_ref[...].reshape(2048, 256)).astype(BF)
    for d in range(4):
        out_ref[d, :, 0:256] = columns
        out_ref[d, :, 256:1280] = d_out


def dense_body(who, *refs):
    in_ref, out_ref, crs_ref, dout_ref, w1_ref, w2_ref = refs[8:]
    for ref, x, c in placed(who, refs):
        for z in range(2):
            for j in range(4):
                w1_ref[x, z, c, :, j * 256 : j * 256 + 256] = ref[j, z]
                w2_ref[x, z, c, :, j * 256 : j * 256 + 256] = ref[j + 4, z]
    w1 = w1_ref[...].reshape(1024, 1024)
    w2 = w2_ref[...].reshape(1024, 1024)
    parts = [in_ref[j, :, 0:256].astype(F32) for j in range(4)]
    centers, scale = norm_parts(parts, 1024)
    for j in range(4):
        crs_ref[:, j * 256 : j * 256 + 256] = in_ref[j, :, 0:256]
    normed = jnp.concatenate([(c * scale).astype(BF) for c in centers], 1)
    d_out = (
        in_ref[0, :, 256:1280].astype(F32)
        + in_ref[1, :, 256:1280].astype(F32)
        + in_ref[2, :, 256:1280].astype(F32)
        + in_ref[3, :, 256:1280].astype(F32)
    ).astype(BF)
    dout_ref[...] = d_out
    inner = dot(normed, w1).astype(BF).astype(F32)
    d_act = dot(d_out, w2).astype(BF).astype(F32)
    rate = 0.7978845608028654
    t = jnp.tanh(rate * (inner + 0.044715 * (inner * inner * inner)))
    share = 0.5 * (1.0 + t)
    act = (inner * share).astype(BF)
    slope = share + 0.5 * inner * (1.0 - t * t) * rate * (1.0 + 0.134145 * (inner * inner))
    d_inner = (d_act * slope).astype(BF)
    d_norm = dot(d_inner, w1, 1, 1).astype(BF)
    outer = dot(act, w2, 1, 1).astype(BF)
    for d in range(4):
        out_ref[d, 0:128] = d_norm
        out_ref[d, 128:160] = outer[d * 32 : d * 32 + 32]


def coarse_back_body(who, recv_ref, crs_ref, dout_ref, w_ref, out_ref, cols_ref):
    me = who[0]
    coarse = crs_ref[...].astype(F32)
    d_norm = (
        recv_ref[0, 0:128].astype(F32)
        + recv_ref[1, 0:128].astype(F32)
        + recv_ref[2, 0:128].astype(F32)
        + recv_ref[3, 0:128].astype(F32)
    )
    d_norm = d_norm.astype(BF).astype(F32)
    (center,), scale = norm_parts([coarse], 1024)
    (d_c,) = norm_back([d_norm], [center], scale, 1024)
    d_coarse = (dout_ref[...].astype(F32) + d_c.astype(BF).astype(F32)).astype(BF)
    for j in range(4):
        cols_ref[j] = d_coarse[:, j * 256 : j * 256 + 256]
    part = dot(cols_ref[me], w_ref[...], 1, 1).astype(BF)
    own = crs_ref[pl.ds(pl.multiple_of(me * 32, 32), 32), :].astype(F32)
    outer = (
        recv_ref[0, 128:160].astype(F32)
        + recv_ref[1, 128:160].astype(F32)
        + recv_ref[2, 128:160].astype(F32)
        + recv_ref[3, 128:160].astype(F32)
    )
    coarse_out = (own + outer).astype(BF)
    for d in range(4):
        out_ref[d, :, 0:2048] = part[d * 32 : d * 32 + 32]
        out_ref[d, :, 2048:3072] = coarse_out


def hidden_back_body(who, recv_ref, hid_ref, g_ref, out_ref):
    half = jnp.bitwise_and(who[0], 1)
    first, second = 2 * half + 1, jnp.bitwise_and(2 * half + 2, 3)
    parts, grads = [], []
    for ab in range(4):
        lanes = slice(ab * 512, ab * 512 + 512)
        total = (
            recv_ref[0, :, lanes].astype(F32)
            + recv_ref[1, :, lanes].astype(F32)
            + recv_ref[2, :, lanes].astype(F32)
            + recv_ref[3, :, lanes].astype(F32)
        )
        grads.append(total.astype(BF).astype(F32))
        parts.append(hid_ref[ab * 32 : ab * 32 + 32].astype(F32))
    centers, scale = norm_parts(parts, 2048)
    back = norm_back(grads, centers, scale, 2048)
    for ab in range(4):
        lanes = slice(ab * 512, ab * 512 + 512)
        for sp, source in ((0, first), (1, second)):
            rows = slice(ab * 32 + sp * 16, ab * 32 + sp * 16 + 16)
            g = g_ref[source, 40:56, lanes].astype(F32)
            b = back[ab][sp * 16 : sp * 16 + 16].astype(BF).astype(F32)
            out_ref[rows, :] = (g + b).astype(BF)


def expand_body(who, recv_ref, hid_ref, w_ref, out_ref):
    coarse_out = recv_ref[:, :, 2048:3072].reshape(128, 1024)
    expanded = dot(coarse_out, w_ref[...]).astype(BF)
    for m in range(4):
        strip = (m + 3) % 4
        for ih in range(2):
            row = (ih * 2 + strip // 2) * 32 + (strip % 2) * 16
            out_ref[m, ih * 16 : ih * 16 + 16, :] = expanded[row : row + 16]
    send_strips(hid_ref[...], who[0], out_ref, 32)


def output_body(who, recv_ref, out_ref):
    half = lax.shift_right_logical(jnp.bitwise_and(who[0] + 3, 3), 1)
    for ih in range(2):
        for ab in range(4):
            hidden = recv_ref[ih * 2 + half, 32 + ab * 16 : 32 + ab * 16 + 16, :]
            added = recv_ref[ab, ih * 16 : ih * 16 + 16, :]
            row = (ih * 4 + ab) * 16
            out_ref[row : row + 16, :] = (hidden.astype(F32) + added.astype(F32)).astype(BF)


def pick(index, source):
    chosen = index[:, None] == jnp.arange(source.shape[0], dtype=jnp.int32)[None]
    return jnp.dot(chosen.astype(BF), source, preferred_element_type=F32).astype(BF)


def grid_of(*sizes):
    return [a.reshape(-1) for a in np.indices(sizes, dtype=np.int32)]


def whole_step(x, qk, wv, wo, scales, w_merge, w_first, w_second, w_expand, g):
    lat = lax.axis_index("lat")
    lats = lax.axis_size("lat")
    core = lax.axis_index("core")
    me = lax.axis_index("mp")
    lons = lax.axis_size(LON)
    who = jnp.stack([me, lat, core, lats, lax.axis_index("x")]).astype(jnp.int32)

    x_flat = x.reshape(512, 512)
    g_flat = g.reshape(128, 512)
    rows = jnp.concatenate(
        [x_flat[0:64], x_flat[256:320], g_flat[0:16], g_flat[64:80]], 0
    )
    rows = lax.ppermute(rows, "lat", [(i, (i - 1) % lats) for i in range(lats)])
    source = jnp.concatenate([x_flat, rows[0:128], g_flat, rows[128:160]], 0)
    ih, a, b, lv, i4, j2 = grid_of(2, 2, 2, 2, 4, 2)
    r, c = ih * 8 + i4 * 2 + a, j2 * 2 + b
    from_g = np.where(r < 12, 640 + lv * 64 + (r + 4) * 4 + c, 768 + lv * 16 + (r - 12) * 4 + c)
    from_x = np.where(r < 12, lv * 256 + (r + 4) * 16 + c, 512 + lv * 64 + (r - 12) * 16 + c)
    sent = pick(jnp.where(me == 0, from_g, from_x), source)
    came = lax.ppermute(sent, LON, [(i, (i - 1) % lons) for i in range(lons)])
    g_strip = jnp.where(me == 0, came, pick(jnp.asarray(from_g), source))
    a, b, sp, lv, i4, j2 = grid_of(2, 2, 2, 2, 4, 2)
    r = (me // 2) * 8 + i4 * 2 + a
    c = 4 + (me % 2) * 8 + sp * 4 + j2 * 2 + b
    near = jnp.where(r < 12, lv * 256 + (r + 4) * 16 + c, 512 + lv * 64 + (r - 12) * 16 + c)
    far = 640 + (me // 2) * 64 + (a * 2 + b) * 16 + lv * 8 + i4 * 2 + j2
    x_win = pick(
        jnp.where(c < 16, near, far), jnp.concatenate([x_flat, rows[0:128], came], 0)
    )

    wo_rows = jnp.concatenate([wo[:, j * 128 : j * 128 + 128] for j in range(4)], 0)
    qkvo = [jnp.concatenate([qk[:, 0], qk[:, 1], wv, wo_rows], 1)]
    for step in STEPS[1:]:
        qkvo.append(lax.ppermute(qkvo[0], "mp", [(i, (i + step) % 4) for i in range(4)]))

    shards = call(pieces_body, arr(16, 96, 256), n_scalar=1, n_in=4)(
        who, w_merge, w_first, w_second, w_expand
    )
    shards = swap(shards, ("lat", "zh"))
    shards = shards.reshape(lats, 2, 96, 256)

    def gathered(own):
        parts = []
        for step in STEPS:
            part = own
            if step:
                part = lax.ppermute(own, "x", [(i, (i + step) % 4) for i in range(4)])
            parts += [part, lax.ppermute(part, "core", [(0, 1), (1, 0)])]
        return parts

    one_parts = gathered(shards[:, :, 0:32])
    two_parts = gathered(shards[:, :, 32:96])

    hidden, merged, stacked = call(
        forward_body,
        [arr(128, 512), arr(4, 56, 2048), arr(4, 128, 384)],
        [pltpu.VMEM((4, 128, 512), BF), pltpu.VMEM((4, 128, 128), BF)],
        n_scalar=2,
        n_in=6,
    )(who, scales, x_win, *qkvo, g_strip)
    merged = swap(merged, "mp")
    merge_full, expand_full, columns = call(
        merge_body,
        [arr(4, 2, 2, 128, 256), arr(4, 2, 2, 64, 512), arr(4, 128, 1280)],
        n_scalar=1,
        n_in=9,
    )(who, *one_parts, merged)
    merge_full = merge_full.reshape(2048, 256)
    expand_full = expand_full.reshape(1024, 512)
    columns = swap(columns, "mp")
    sums, coarse, d_out = call(
        dense_body,
        [arr(4, 160, 1024), arr(128, 1024), arr(128, 1024)],
        [pltpu.VMEM((4, 2, 2, 64, 1024), BF), pltpu.VMEM((4, 2, 2, 64, 1024), BF)],
        n_scalar=1,
        n_in=9,
    )(who, *two_parts, columns)
    sums = swap(sums, "mp")
    merges = call(
        coarse_back_body,
        arr(4, 32, 3072),
        [pltpu.VMEM((4, 128, 256), BF)],
        n_scalar=1,
        n_in=4,
    )(who, sums, coarse, d_out, merge_full)
    merges = swap(merges, "mp")
    d_hidden = call(hidden_back_body, arr(128, 512), n_scalar=1, n_in=3)(
        who, merges, hidden, merged
    )
    grads = call(
        backward_body,
        arr(4, 64, 512),
        [pltpu.VMEM((4, 128, 512), BF), pltpu.VMEM((128, 512), F32)],
        n_scalar=2,
        n_in=7,
    )(who, scales, x_win, d_hidden, stacked, *qkvo)
    added = call(expand_body, arr(4, 96, 512), n_scalar=1, n_in=3)(
        who, merges, hidden, expand_full
    )
    added = swap(added, "mp")
    grads, added = lax.optimization_barrier((grads, added))
    grads = swap(grads, "mp")
    out_strip = call(output_body, arr(128, 512), n_scalar=1, n_in=1)(who, added)
    half = ((me + 3) % 4) // 2
    grad_strip = jnp.concatenate(
        [
            lax.dynamic_index_in_dim(grads, half, 0, False),
            lax.dynamic_index_in_dim(grads, half + 2, 0, False),
        ],
        0,
    )

    across = [(lon * 4, ((lon + 1) % lons) * 4) for lon in range(lons)]
    down = [
        ((la * lons + lon) * 4 + m, (((la + 1) % lats) * lons + (lon + (m == 0)) % lons) * 4 + m)
        for la in range(lats)
        for lon in range(lons)
        for m in range(4)
    ]
    lv, r, c = grid_of(2, 16, 4)
    s = r - 4
    kept = (s // 8) * 64 + ((s % 2) * 2 + c % 2) * 16 + lv * 8 + ((s % 8) // 2) * 2 + c // 2
    tops = np.where(
        r < 4, 256 + ((r % 2) * 2 + c % 2) * 8 + lv * 4 + (r // 2) * 2 + c // 2, 0
    )

    def rolled_back(strip):
        beyond = lax.ppermute(strip, LONMP, across)
        last = strip[64:128].reshape(8, 8, 512)[:, 4:8].reshape(32, 512)
        above = lax.ppermute(last, ALL, down)
        shift = jnp.where(me == 0, 128, 0)
        index = jnp.where(r < 4, tops, kept + shift)
        whole = pick(index, jnp.concatenate([strip, beyond, above], 0))
        return whole.reshape(2, 16, 4, 512)

    return rolled_back(out_strip), rolled_back(grad_strip)


def solution(mesh):
    lats, lons, mps = (mesh.shape[n] for n in ("lat", "lon", "mp"))
    fine = Mesh(
        mesh.devices.reshape(lats, lons // 4, 2, 2, mps), ("lat", "x", "zh", "core", "mp")
    )
    in_specs = (
        P(None, "lat", LON, None),
        P(None, None, "mp"),
        P(None, "mp"),
        P("mp", None),
        P(),
        P(LON, "mp"),
        P(LON, "mp"),
        P("mp", LON),
        P(LON, "mp"),
        P(None, "lat", LONMP, None),
    )
    out_specs = (P(None, "lat", LONMP, None), P(None, "lat", LONMP, None))
    return jax.shard_map(
        whole_step, mesh=fine, in_specs=in_specs, out_specs=out_specs, check_vma=False
    )
```
